32 devices in a mesh: dp: 2 (over y), expert: 16 (over z, x, core).
Axes of the slice: x: 2, y: 2, z: 4, core: 2. Of those that a mesh axis runs over, the one named last changes fastest.
Arguments:
- tokens: bfloat16 [4096, 1024], P(('dp', 'expert')), may hold values from -6 to 6
- segments: int32 [4096], P(('dp', 'expert')), may hold values from 0 to 127, never falling along the last dimension, each value on 1 to 128 neighbouring positions
- routes: int32 [4096, 8], P(('dp', 'expert')), may hold values from 0 to 15, all different within a row; in each aligned block of 128 rows (0 to 127, 128 to 255, ...) at most 80 rows name the same one
- first_gain: bfloat16 [1024], P('dp'), may hold values from 0.5 to 1.5
- query_weight: bfloat16 [1024, 1024], P('dp'), may hold values from -0.75 to 0.75
- key_projection_weight: bfloat16 [1024, 512], P('dp'), may hold values from -0.75 to 0.75
- value_projection_weight: bfloat16 [1024, 512], P('dp'), may hold values from -0.1875 to 0.1875
- out_weight: bfloat16 [1024, 1024], P('dp'), may hold values from -0.75 to 0.75
- second_gain: bfloat16 [1024], P('dp'), may hold values from 0.5 to 1.5
- router_weight: bfloat16 [1024, 16], P('dp'), may hold values from -0.375 to 0.375
- gate_weight: bfloat16 [16, 1024, 512], P('expert'), may hold values from -0.1875 to 0.1875
- up_weight: bfloat16 [16, 1024, 512], P('expert'), may hold values from -0.1875 to 0.1875
- down_weight: bfloat16 [16, 512, 1024], P('expert'), may hold values from -0.5 to 0.5
- cotangent: bfloat16 [4096, 1024], P(('dp', 'expert')), may hold values from -6 to 6
Outputs:
- output: bfloat16 [4096, 1024], P(('dp', 'expert'))
- grad_tokens: float32 [4096, 1024], P(('dp', 'expert'))
- first_gain_grad: float32 [1024], P('dp')
- query_weight_grad: float32 [1024, 1024], P('dp')
- key_weight_grad: float32 [1024, 512], P('dp')
- value_weight_grad: float32 [1024, 512], P('dp')
- out_weight_grad: float32 [1024, 1024], P('dp')
- second_gain_grad: float32 [1024], P('dp')
- router_weight_grad: float32 [1024, 16], P('dp')
- gate_weight_grad: float32 [16, 1024, 512], P('expert', 'dp')
- up_weight_grad: float32 [16, 1024, 512], P('expert', 'dp')
- down_weight_grad: float32 [16, 512, 1024], P('expert', None, 'dp')
The draws below stay inside these ranges and needn't reach their ends.
Inputs may be any that keep to these rules, and one draw needn't show every extreme that they name: `routes`: within the rows of one device (aligned blocks of 128 tokens) no expert is named by more than 80 rows; in some block one expert is named by exactly 80. A row names 8 different experts. `segments`: segment numbers never fall along the tokens; a segment holds 1 to 128 tokens and one holds exactly 128.
All inputs are finite; a program needn't handle non-finite values.
Results may differ from the reference program's by a relative error of at most 0.02.
The reference program's roundings to bfloat16 on the way count: a program that leaves them out, or rounds other values in their place, can miss the bound.
Values may be sent and summed in bfloat16 or wider, within the bound.
A program may use at most 128 MiB of HBM per device.

```python
import math
import jax
import jax.numpy as jnp
import numpy as np
from jax import lax

MODEL_DIM = 1024
QUERY_HEADS = 16
KEY_VALUE_HEADS = 8
HEAD_DIM = 64
FF = 512
TOPK = 8
SEQUENCE_LENGTH = 128
TOK_DEV = 128
TOKENS = 4096
EXPERTS = 16
CAP = 80
N_DP = 2
N_EXPERT = 16


def level_of(key, dims, cuts, smallest, largest):
    gain = 1.0
    for axis_at, parts in cuts:
        draws = jax.random.uniform(jax.random.fold_in(jax.random.fold_in(key, 6), axis_at), (parts,), jnp.float32, smallest / len(cuts), largest / len(cuts))
        gain = gain * jnp.repeat(jnp.exp(draws), dims[axis_at] // parts).reshape((-1,) + (1,) * (len(dims) - 1 - axis_at))
    return gain


def split_up(amount, total, reach, skew):
    portions = [(1 << 20) // math.isqrt(grade ** skew) + 1 for grade in range(2, amount + 1)]
    surplus, holding = total - reach - (amount - 1), [1] * (amount - 1)
    while surplus > 0:
        free = [i for i in range(amount - 1) if holding[i] < reach]
        pool, left = sum([portions[i] for i in free]), surplus
        for i in free:
            addition = min(reach - holding[i], max(1, left * portions[i] // pool), surplus)
            holding[i] = holding[i] + addition
            surplus = surplus - addition
    return np.array([reach] + holding)


def uneven(stream_key, count, total, limit, slope):
    if count == 2:
        one = jax.random.randint(stream_key, (), max(1, total - limit), min(limit, total - 1) + 1)
        return jnp.stack([one, total - one])
    sizes = jnp.asarray(split_up(count, total, limit, slope), jnp.int32)
    couples = (count - 1) // 2
    donor, receiver = sizes[1:1 + 2 * couples:2], sizes[2:2 + 2 * couples:2]
    slack = jnp.minimum(donor - 1, limit - receiver)
    moved = jax.random.randint(jax.random.fold_in(stream_key, 1), (couples,), 0, 1 << 20) % (slack + 1)
    sizes = sizes.at[1:1 + 2 * couples:2].set(donor - moved).at[2:2 + 2 * couples:2].set(receiver + moved)
    return sizes[jax.random.permutation(jax.random.fold_in(stream_key, 2), count)]


def assign_block(own_key, own, number, rows, amount, top, bound, skew):
    order = jax.random.permutation(own_key, amount)
    packed, ordinary = load_shares(amount, rows * top, bound, skew, True), load_shares(amount, rows * top, bound, skew, False)
    places = jnp.arange(amount)

    def named(sizes, offset_by):
        used = int((sizes > 0).sum())
        fixed = max(1, used // 4)
        moved = fixed + (places - fixed + offset_by * (used - fixed)) % max(1, amount - fixed)
        return jnp.zeros((amount,), jnp.int32).at[order[jnp.where(places < fixed, places, moved)]].set(jnp.asarray(sizes, jnp.int32))

    sizes = jnp.where(number % 4 == 0, named(packed, number // 4), named(ordinary, number - number // 4 - 1))
    mixed = jax.random.permutation(jax.random.fold_in(own, 3), amount)
    giver, taker = mixed[0:amount // 2 * 2:2], mixed[1:amount // 2 * 2:2]
    slack = jnp.minimum(sizes[giver] - 1, bound - sizes[taker]) // 2
    slack = jnp.where((giver == order[0]) | (taker == order[0]) | (sizes[taker] == 0), 0, jnp.maximum(slack, 0))
    moved = jax.random.randint(jax.random.fold_in(own, 4), (amount // 2,), 0, 1 << 20) % (slack + 1)
    sizes = sizes.at[giver].add(-moved).at[taker].add(moved)
    labels = jnp.searchsorted(jnp.cumsum(sizes), jnp.arange(rows * top), side="right").astype(jnp.int32)
    table = labels.reshape(top, rows).T
    table = table[jax.random.permutation(jax.random.fold_in(own, 1), rows)]
    offset_by = jax.random.randint(jax.random.fold_in(own, 2), (rows, 1), 0, top)
    return jnp.take_along_axis(table, (jnp.arange(top)[None, :] + offset_by) % top, axis=1)


def load_shares(number_of, total, reach, skew, full):
    loads = [(1 << 20) // math.isqrt(rank ** skew) + 1 for rank in range(1, number_of + 1)]
    largest = reach if full else min(reach, max(-(-total // number_of), total * loads[0] // sum(loads)))
    least = 1 if total - largest >= number_of - 1 else 0
    holding, surplus = [largest] + [least] * (number_of - 1), total - largest - least * (number_of - 1)
    while surplus > 0:
        movable = [i for i in range(1, number_of) if holding[i] < largest] or [i for i in range(1, number_of) if holding[i] < reach]
        mass, budget = sum([loads[i] for i in movable]), surplus
        for i in movable:
            addition = min(reach - holding[i], max(1, budget * loads[i] // mass), surplus)
            holding[i] = holding[i] + addition
            surplus = surplus - addition
    return np.array(holding)


def gaussian(own_key, shape, width, most, shards=(), kind=jnp.bfloat16):
    values = jax.random.normal(own_key, shape, jnp.float32) * width
    if len(shards) > 0:
        values = level_of(own_key, shape, shards, -0.22, 0.18) * values
    return jnp.clip(values, min=-most, max=most).astype(kind)


def setup_inputs(seed: int = 0) -> dict:
    seeds = jax.random.split(jax.random.key(seed), 15)
    tokens = gaussian(seeds[0], (TOKENS, MODEL_DIM), 1.0, 6.0, ((0, 32),))
    segments = jnp.searchsorted(jnp.cumsum(uneven(seeds[1], TOKENS // (SEQUENCE_LENGTH // 4), TOKENS, SEQUENCE_LENGTH, 0)), jnp.arange(TOKENS), side="right").astype(jnp.int32)
    routes_keys = jax.random.split(jax.random.fold_in(seeds[2], 1), TOKENS // TOK_DEV)
    routes_turns = jax.random.permutation(jax.random.fold_in(seeds[2], 3), TOKENS // TOK_DEV)
    routes = jax.vmap(lambda own, number: assign_block(jax.random.fold_in(seeds[2], 2), own, number, TOK_DEV, EXPERTS, TOPK, CAP, 1))(routes_keys, routes_turns).reshape((TOKENS, TOPK))
    first_gain = jnp.clip(1.0 + 0.1 * jax.random.normal(seeds[3], (MODEL_DIM,), jnp.float32), 0.5, 1.5).astype(jnp.bfloat16)
    query_weight = gaussian(seeds[4], (MODEL_DIM, QUERY_HEADS * HEAD_DIM), (MODEL_DIM // 16) ** -0.5, 0.75, ((0, 2),))
    key_projection_weight = gaussian(seeds[5], (MODEL_DIM, KEY_VALUE_HEADS * HEAD_DIM), (MODEL_DIM // 16) ** -0.5, 0.75, ((0, 2),))
    value_projection_weight = gaussian(seeds[6], (MODEL_DIM, KEY_VALUE_HEADS * HEAD_DIM), MODEL_DIM ** -0.5, 0.1875, ((0, 2),))
    out_weight = gaussian(seeds[7], (QUERY_HEADS * HEAD_DIM, MODEL_DIM), (QUERY_HEADS * HEAD_DIM // 16) ** -0.5, 0.75, ((0, 2),))
    second_gain = jnp.clip(1.0 + 0.1 * jax.random.normal(seeds[8], (MODEL_DIM,), jnp.float32), 0.5, 1.5).astype(jnp.bfloat16)
    router_weight = gaussian(seeds[9], (MODEL_DIM, EXPERTS), (MODEL_DIM // 4) ** -0.5, 0.375, ((0, 2),))
    gate_weight = gaussian(seeds[10], (EXPERTS, MODEL_DIM, FF), MODEL_DIM ** -0.5, 0.1875, ((0, 16),))
    up_weight = gaussian(seeds[11], (EXPERTS, MODEL_DIM, FF), MODEL_DIM ** -0.5, 0.1875, ((0, 16),))
    down_weight = gaussian(seeds[12], (EXPERTS, FF, MODEL_DIM), (FF // 4) ** -0.5, 0.5, ((0, 16),))
    cotangent = gaussian(seeds[13], (TOKENS, MODEL_DIM), 1.0, 6.0, ((0, 32),))
    return {"tokens": tokens, "segments": segments, "routes": routes, "first_gain": first_gain, "query_weight": query_weight, "key_projection_weight": key_projection_weight, "value_projection_weight": value_projection_weight, "out_weight": out_weight, "second_gain": second_gain, "router_weight": router_weight, "gate_weight": gate_weight, "up_weight": up_weight, "down_weight": down_weight, "cotangent": cotangent}


EPSILON = 1e-06
SCORE_SCALE = 0.015625
ROPE_BASE = 10000.0
MASKED = -1e+30

def product(pattern, left_op, right_op):
    return jnp.einsum(pattern, left_op.astype(jnp.float32), right_op.astype(jnp.float32))

def matrix_multiply(left_op, right_op):
    return jnp.dot(left_op, right_op, preferred_element_type=jnp.float32)

def rope_tables(seq_len, head_size):
    positions = jnp.arange(seq_len, dtype=jnp.float32)
    exponent = jnp.arange(head_size // 2, dtype=jnp.float32) * (2.0 / head_size)
    angles = positions[:, None] * (ROPE_BASE ** (-exponent))[None, :]
    return (jnp.cos(angles)[None, :, None, :], jnp.sin(angles)[None, :, None, :])

def apply_rotary(values, cosine_table, sine_table):
    middle = values.shape[-1] // 2
    first_half = values[..., :middle]
    second_half = values[..., middle:]
    return jnp.concatenate([first_half * cosine_table - second_half * sine_table, second_half * cosine_table + first_half * sine_table], -1)

def inverse_rotary(gradient, cosine_table, sine_table):
    middle = gradient.shape[-1] // 2
    first_half = gradient[..., :middle]
    second_half = gradient[..., middle:]
    return jnp.concatenate([first_half * cosine_table + second_half * sine_table, second_half * cosine_table - first_half * sine_table], -1)

def normalize(values, gain_vec):
    factor = lax.rsqrt(lax.optimization_barrier(jnp.mean(values * values, -1, keepdims=True)) + EPSILON)
    normed = values * factor
    return (normed, factor, (normed * gain_vec).astype(jnp.bfloat16))

def normalize_back(gradient, normed, factor, gain_vec):
    gain_grad = lax.optimization_barrier(jnp.sum(gradient * normed, 0))
    scaled = gradient * gain_vec
    return (factor * (scaled - normed * lax.optimization_barrier(jnp.mean(scaled * normed, -1, keepdims=True))), gain_grad)

def segment_mask(segments):
    seq_len = segments.shape[1]
    causal = jnp.arange(seq_len)[:, None] >= jnp.arange(seq_len)[None, :]
    same_doc = segments[:, :, None] == segments[:, None, :]
    return (same_doc & causal[None])[:, None, None]

def score_table(query_rows, key_row_block, mask_tab):
    raw_scores = product('sqhgw,skhw->shgqk', query_rows, key_row_block) * SCORE_SCALE
    return jnp.where(mask_tab, raw_scores, MASKED)

def mixer_forward(tokens, segments, gain_vec, query_mat, key_matrix, value_matrix, out_mat):
    token_rows = tokens.shape[0]
    local_sequences = token_rows // SEQUENCE_LENGTH
    query_groups = QUERY_HEADS // KEY_VALUE_HEADS
    cosine_table, sine_table = rope_tables(SEQUENCE_LENGTH, HEAD_DIM)
    mask_tab = segment_mask(segments.reshape(local_sequences, SEQUENCE_LENGTH))
    residual = tokens.astype(jnp.float32)
    normed, factor, attention_input = normalize(residual, gain_vec)
    query_rows = apply_rotary(matrix_multiply(attention_input, query_mat).reshape(local_sequences, SEQUENCE_LENGTH, QUERY_HEADS, HEAD_DIM), cosine_table, sine_table)
    query_rows = query_rows.astype(jnp.bfloat16).reshape(local_sequences, SEQUENCE_LENGTH, KEY_VALUE_HEADS, query_groups, HEAD_DIM)
    key_row_block = apply_rotary(matrix_multiply(attention_input, key_matrix).reshape(local_sequences, SEQUENCE_LENGTH, KEY_VALUE_HEADS, HEAD_DIM), cosine_table, sine_table).astype(jnp.bfloat16)
    value_row_block = matrix_multiply(attention_input, value_matrix).astype(jnp.bfloat16).reshape(local_sequences, SEQUENCE_LENGTH, KEY_VALUE_HEADS, HEAD_DIM)
    scores = score_table(query_rows, key_row_block, mask_tab)
    row_peak = lax.optimization_barrier(jnp.max(scores, -1, keepdims=True))
    logsum = row_peak + jnp.log(lax.optimization_barrier(jnp.sum(jnp.exp(scores - row_peak), -1, keepdims=True)))
    weights = jnp.exp(scores - logsum).astype(jnp.bfloat16)
    attended = product('shgqk,skhw->sqhgw', weights, value_row_block).astype(jnp.bfloat16)
    hidden = residual + matrix_multiply(attended.reshape(token_rows, QUERY_HEADS * HEAD_DIM), out_mat)
    saved = (normed, factor, attention_input, query_rows, key_row_block, value_row_block, attended, logsum, mask_tab, cosine_table, sine_table)
    return (hidden, saved)

def mixer_backward(grad_hidden, saved, gain_vec, query_mat, key_matrix, value_matrix, out_mat):
    normed, factor, attention_input, query_rows, key_row_block, value_row_block, attended, logsum, mask_tab, cosine_table, sine_table = saved
    token_rows = grad_hidden.shape[0]
    local_sequences = token_rows // SEQUENCE_LENGTH
    grad_round = grad_hidden.astype(jnp.bfloat16)
    out_grad = matrix_multiply(attended.reshape(token_rows, QUERY_HEADS * HEAD_DIM).T, grad_round)
    grad_attended = matrix_multiply(grad_round, out_mat.T).astype(jnp.bfloat16).reshape(query_rows.shape)
    scores = score_table(query_rows, key_row_block, mask_tab)
    prob_full = jnp.exp(scores - logsum)
    values_gradient = product('shgqk,sqhgw->skhw', prob_full.astype(jnp.bfloat16), grad_attended)
    grad_weights = product('sqhgw,skhw->shgqk', grad_attended, value_row_block)
    row_delta = product('sqhgw,sqhgw->shgq', grad_attended, attended)[..., None]
    grad_scores = (prob_full * (grad_weights - row_delta) * SCORE_SCALE).astype(jnp.bfloat16)
    grad_queries = product('shgqk,skhw->sqhgw', grad_scores, key_row_block)
    keys_gradient = product('shgqk,sqhgw->skhw', grad_scores, query_rows)
    query_grad = inverse_rotary(grad_queries.reshape(local_sequences, SEQUENCE_LENGTH, QUERY_HEADS, HEAD_DIM), cosine_table, sine_table)
    query_grad = query_grad.astype(jnp.bfloat16).reshape(token_rows, QUERY_HEADS * HEAD_DIM)
    key_gradient = inverse_rotary(keys_gradient, cosine_table, sine_table).astype(jnp.bfloat16).reshape(token_rows, KEY_VALUE_HEADS * HEAD_DIM)
    value_gradient = values_gradient.astype(jnp.bfloat16).reshape(token_rows, KEY_VALUE_HEADS * HEAD_DIM)
    query_wgrad = matrix_multiply(attention_input.T, query_grad)
    key_wgrad = matrix_multiply(attention_input.T, key_gradient)
    value_wgrad = matrix_multiply(attention_input.T, value_gradient)
    grad_attn_input = matrix_multiply(query_grad, query_mat.T) + matrix_multiply(key_gradient, key_matrix.T) + matrix_multiply(value_gradient, value_matrix.T)
    grad_normed, gain_grad = normalize_back(grad_attn_input, normed, factor, gain_vec)
    return (grad_hidden + grad_normed, gain_grad, query_wgrad, key_wgrad, value_wgrad, out_grad)

def route_weights(expert_input, router_mat, routes):
    logits = matrix_multiply(expert_input, router_mat)
    chosen_hot = (routes[:, :, None] == jnp.arange(router_mat.shape[1], dtype=jnp.int32)[None, None, :]).astype(jnp.float32)
    chosen = lax.optimization_barrier(jnp.sum(chosen_hot * logits[:, None, :], -1))
    return (jax.nn.softmax(chosen, -1), chosen_hot)

def route_back(route_prob, grad_prob, chosen_hot):
    grad_chosen = route_prob * (grad_prob - lax.optimization_barrier(jnp.sum(route_prob * grad_prob, -1, keepdims=True)))
    return lax.optimization_barrier(jnp.sum(chosen_hot * grad_chosen[:, :, None], 1)).astype(jnp.bfloat16)

def expert_forward(owner_rows, gate_mat, up_mat, down_mat):
    gate_pre = product('erd,edf->erf', owner_rows, gate_mat)
    up_pre = product('erd,edf->erf', owner_rows, up_mat)
    gate_sig = jax.nn.sigmoid(gate_pre)
    gate_act = gate_pre * gate_sig
    inner_acts = (gate_act * up_pre).astype(jnp.bfloat16)
    expert_out = product('erf,efd->erd', inner_acts, down_mat).astype(jnp.bfloat16)
    return (expert_out, (gate_pre, up_pre, gate_sig, gate_act, inner_acts))

def expert_backward(grad_rows, owner_rows, kept_acts, gate_mat, up_mat, down_mat):
    gate_pre, up_pre, gate_sig, gate_act, inner_acts = kept_acts
    grad_inner = product('erd,efd->erf', grad_rows, down_mat)
    down_grad = product('erf,erd->efd', inner_acts, grad_rows)
    silu_slope = gate_sig * (1.0 + gate_pre * (1.0 - gate_sig))
    grad_gate = (grad_inner * up_pre * silu_slope).astype(jnp.bfloat16)
    grad_up = (grad_inner * gate_act).astype(jnp.bfloat16)
    gate_grad = product('erd,erf->edf', owner_rows, grad_gate)
    up_grad = product('erd,erf->edf', owner_rows, grad_up)
    grad_owner_rows = product('erf,edf->erd', grad_gate, gate_mat) + product('erf,edf->erd', grad_up, up_mat)
    return (grad_owner_rows.astype(jnp.bfloat16), gate_grad, up_grad, down_grad)

def reference(tokens, segments, routes, first_gain, query_weight, key_projection_weight, value_projection_weight, out_weight, second_gain, router_weight, gate_weight, up_weight, down_weight, cotangent):
    device_count = N_DP * N_EXPERT
    total_seqs = TOKENS // SEQUENCE_LENGTH
    block_seqs = math.gcd(total_seqs, max(1, 4096 // SEQUENCE_LENGTH))
    block_count = total_seqs // block_seqs
    tok_blocks = tokens.reshape(block_count, block_seqs * SEQUENCE_LENGTH, MODEL_DIM)
    seg_blocks = segments.reshape(block_count, block_seqs * SEQUENCE_LENGTH)

    def forward_block(running, pieces):
        hidden_piece, saved = mixer_forward(pieces[0], pieces[1], first_gain, query_weight, key_projection_weight, value_projection_weight, out_weight)
        return (running, hidden_piece)
    unused, hidden_blocks = lax.scan(forward_block, jnp.zeros((), jnp.float32), (tok_blocks, seg_blocks))
    hidden = hidden_blocks.reshape(TOKENS, MODEL_DIM)
    normed_second, factor_second, expert_input = normalize(hidden, second_gain)
    route_prob, chosen_hot = route_weights(expert_input, router_weight, routes)
    flat_routes = routes.reshape(device_count, TOK_DEV * TOPK)
    route_hot = (flat_routes[..., None] == jnp.arange(EXPERTS, dtype=jnp.int32)[None, None, :]).astype(jnp.int32)
    slot_of = lax.optimization_barrier(jnp.sum(route_hot * jnp.cumsum(route_hot, 1), -1)) - 1
    device_rows = jnp.arange(device_count, dtype=jnp.int32)[:, None]
    target = (flat_routes * (device_count * CAP) + device_rows * CAP + slot_of).reshape(-1).astype(jnp.int32)
    slot_table = jnp.full((EXPERTS * device_count * CAP,), -1, jnp.int32)
    slot_table = slot_table.at[target].set(jnp.arange(TOKENS * TOPK, dtype=jnp.int32))
    slot_table = slot_table.reshape(EXPERTS, device_count * CAP)
    grad_output = cotangent.astype(jnp.float32)
    flat_prob = route_prob.reshape(-1)

    def expert_step(running, pieces):
        mixture, grad_expert_input, grad_prob = running
        gate_slice, up_slice, down_slice, entries = pieces
        live_slot = entries >= 0
        source = jnp.maximum(entries, 0)
        token_of = source // TOPK
        owner_rows = jnp.where(live_slot[:, None], expert_input[token_of], jnp.zeros((), jnp.bfloat16))[None]
        expert_out, kept_acts = expert_forward(owner_rows, gate_slice[None], up_slice[None], down_slice[None])
        out_rows = expert_out[0].astype(jnp.float32)
        weight_rows = jnp.where(live_slot, flat_prob[source], 0.0)
        mixture = mixture.at[token_of].add(weight_rows[:, None] * out_rows)
        grad_prob = grad_prob.at[source].add(jnp.where(live_slot, lax.optimization_barrier(jnp.sum(grad_output[token_of] * out_rows, -1)), 0.0))
        grad_rows = (weight_rows[:, None] * grad_output[token_of]).astype(jnp.bfloat16)[None]
        grad_owner_rows, gate_grad, up_grad, down_grad = expert_backward(grad_rows, owner_rows, kept_acts, gate_slice[None], up_slice[None], down_slice[None])
        grad_expert_input = grad_expert_input.at[token_of].add(jnp.where(live_slot[:, None], grad_owner_rows[0].astype(jnp.float32), 0.0))
        return ((mixture, grad_expert_input, grad_prob), (gate_grad[0], up_grad[0], down_grad[0]))
    start = (jnp.zeros((TOKENS, MODEL_DIM), jnp.float32), jnp.zeros((TOKENS, MODEL_DIM), jnp.float32), jnp.zeros((TOKENS * TOPK,), jnp.float32))
    finals, expert_grads = lax.scan(expert_step, start, (gate_weight, up_weight, down_weight, slot_table))
    mixture, grad_expert_input, grad_prob = finals
    output = (hidden + mixture).astype(jnp.bfloat16)
    router_grad = route_back(route_prob, grad_prob.reshape(TOKENS, TOPK), chosen_hot)
    grad_expert_input = grad_expert_input + matrix_multiply(router_grad, router_weight.T)
    router_wgrad = matrix_multiply(expert_input.T, router_grad)
    grad_normed, second_gain_grad = normalize_back(grad_expert_input, normed_second, factor_second, second_gain)
    grad_hidden = grad_output + grad_normed
    grad_blocks = grad_hidden.reshape(block_count, block_seqs * SEQUENCE_LENGTH, MODEL_DIM)

    def backward_block(running, pieces):
        tok_piece, seg_piece, grad_piece = pieces
        hidden_piece, saved = mixer_forward(tok_piece, seg_piece, first_gain, query_weight, key_projection_weight, value_projection_weight, out_weight)
        results = mixer_backward(grad_piece, saved, first_gain, query_weight, key_projection_weight, value_projection_weight, out_weight)
        totals = tuple((running[index] + results[index + 1] for index in range(5)))
        return (totals, results[0])
    initial_gradients = (jnp.zeros((MODEL_DIM,), jnp.float32), jnp.zeros((MODEL_DIM, QUERY_HEADS * HEAD_DIM), jnp.float32), jnp.zeros((MODEL_DIM, KEY_VALUE_HEADS * HEAD_DIM), jnp.float32), jnp.zeros((MODEL_DIM, KEY_VALUE_HEADS * HEAD_DIM), jnp.float32), jnp.zeros((QUERY_HEADS * HEAD_DIM, MODEL_DIM), jnp.float32))
    totals, grad_token_blocks = lax.scan(backward_block, initial_gradients, (tok_blocks, seg_blocks, grad_blocks))
    grad_tokens = grad_token_blocks.reshape(TOKENS, MODEL_DIM)
    return (output, grad_tokens, totals[0], totals[1], totals[2], totals[3], totals[4], second_gain_grad, router_wgrad, expert_grads[0], expert_grads[1], expert_grads[2])
```

```python
import jax
import jax.numpy as jnp
from jax import lax
from jax.sharding import PartitionSpec as P

QUERY_HEADS = 16
KEY_VALUE_HEADS = 8
HEAD_DIM = 64
SEQUENCE_LENGTH = 128


EPSILON = 1e-06
SCORE_SCALE = 0.015625
ROPE_BASE = 10000.0
MASKED = -1e30


def product(pattern, left_op, right_op):
    return jnp.einsum(pattern, left_op, right_op, preferred_element_type=jnp.float32)


def matrix_multiply(left_op, right_op):
    return jnp.dot(left_op, right_op, preferred_element_type=jnp.float32)


def rope_tables(seq_len, head_size):
    positions = jnp.arange(seq_len, dtype=jnp.float32)
    exponent = jnp.arange(head_size // 2, dtype=jnp.float32) * (2.0 / head_size)
    angles = positions[:, None] * (ROPE_BASE ** (-exponent))[None, :]
    return (jnp.cos(angles)[None, :, None, :], jnp.sin(angles)[None, :, None, :])


def apply_rotary(values, cosine_table, sine_table):
    middle = values.shape[-1] // 2
    first_half = values[..., :middle]
    second_half = values[..., middle:]
    return jnp.concatenate(
        [
            first_half * cosine_table - second_half * sine_table,
            second_half * cosine_table + first_half * sine_table,
        ],
        -1,
    )


def inverse_rotary(gradient, cosine_table, sine_table):
    middle = gradient.shape[-1] // 2
    first_half = gradient[..., :middle]
    second_half = gradient[..., middle:]
    return jnp.concatenate(
        [
            first_half * cosine_table + second_half * sine_table,
            second_half * cosine_table - first_half * sine_table,
        ],
        -1,
    )


def normalize(values, gain_vec):
    factor = lax.rsqrt(jnp.mean(values * values, -1, keepdims=True) + EPSILON)
    normed = values * factor
    return (normed, factor, (normed * gain_vec).astype(jnp.bfloat16))


def normalize_back(gradient, normed, factor, gain_vec):
    gain_grad = jnp.sum(gradient * normed, 0)
    scaled = gradient * gain_vec
    return (factor * (scaled - normed * jnp.mean(scaled * normed, -1, keepdims=True)), gain_grad)


def segment_mask(segments):
    seq_len = segments.shape[1]
    causal = jnp.arange(seq_len)[:, None] >= jnp.arange(seq_len)[None, :]
    same_doc = segments[:, :, None] == segments[:, None, :]
    return (same_doc & causal[None])[:, None, None]


def score_table(query_rows, key_row_block, mask_tab):
    raw_scores = product("sqhgw,skhw->shgqk", query_rows, key_row_block) * SCORE_SCALE
    return jnp.where(mask_tab, raw_scores, MASKED)


def mixer_forward(tokens, segments, gain_vec, query_mat, key_matrix, value_matrix, out_mat):
    token_rows = tokens.shape[0]
    local_sequences = token_rows // SEQUENCE_LENGTH
    query_groups = QUERY_HEADS // KEY_VALUE_HEADS
    cosine_table, sine_table = rope_tables(SEQUENCE_LENGTH, HEAD_DIM)
    mask_tab = segment_mask(segments.reshape(local_sequences, SEQUENCE_LENGTH))
    residual = tokens.astype(jnp.float32)
    normed, factor, attention_input = normalize(residual, gain_vec)
    query_rows = apply_rotary(
        matrix_multiply(attention_input, query_mat).reshape(
            local_sequences, SEQUENCE_LENGTH, QUERY_HEADS, HEAD_DIM
        ),
        cosine_table,
        sine_table,
    )
    query_rows = query_rows.astype(jnp.bfloat16).reshape(
        local_sequences, SEQUENCE_LENGTH, KEY_VALUE_HEADS, query_groups, HEAD_DIM
    )
    key_row_block = apply_rotary(
        matrix_multiply(attention_input, key_matrix).reshape(
            local_sequences, SEQUENCE_LENGTH, KEY_VALUE_HEADS, HEAD_DIM
        ),
        cosine_table,
        sine_table,
    ).astype(jnp.bfloat16)
    value_row_block = (
        matrix_multiply(attention_input, value_matrix)
        .astype(jnp.bfloat16)
        .reshape(local_sequences, SEQUENCE_LENGTH, KEY_VALUE_HEADS, HEAD_DIM)
    )
    scores = score_table(query_rows, key_row_block, mask_tab)
    row_peak = jnp.max(scores, -1, keepdims=True)
    logsum = row_peak + jnp.log(jnp.sum(jnp.exp(scores - row_peak), -1, keepdims=True))
    weights = jnp.exp(scores - logsum).astype(jnp.bfloat16)
    attended = product("shgqk,skhw->sqhgw", weights, value_row_block).astype(jnp.bfloat16)
    hidden = residual + matrix_multiply(
        attended.reshape(token_rows, QUERY_HEADS * HEAD_DIM), out_mat
    )
    saved = (
        normed,
        factor,
        attention_input,
        query_rows,
        key_row_block,
        value_row_block,
        attended,
        logsum,
        mask_tab,
        cosine_table,
        sine_table,
    )
    return (hidden, saved)


def mixer_backward(grad_hidden, saved, gain_vec, query_mat, key_matrix, value_matrix, out_mat):
    (
        normed,
        factor,
        attention_input,
        query_rows,
        key_row_block,
        value_row_block,
        attended,
        logsum,
        mask_tab,
        cosine_table,
        sine_table,
    ) = saved
    token_rows = grad_hidden.shape[0]
    local_sequences = token_rows // SEQUENCE_LENGTH
    grad_round = grad_hidden.astype(jnp.bfloat16)
    out_grad = matrix_multiply(attended.reshape(token_rows, QUERY_HEADS * HEAD_DIM).T, grad_round)
    grad_attended = (
        matrix_multiply(grad_round, out_mat.T).astype(jnp.bfloat16).reshape(query_rows.shape)
    )
    scores = score_table(query_rows, key_row_block, mask_tab)
    prob_full = jnp.exp(scores - logsum)
    values_gradient = product("shgqk,sqhgw->skhw", prob_full.astype(jnp.bfloat16), grad_attended)
    grad_weights = product("sqhgw,skhw->shgqk", grad_attended, value_row_block)
    row_delta = product("sqhgw,sqhgw->shgq", grad_attended, attended)[..., None]
    grad_scores = (prob_full * (grad_weights - row_delta) * SCORE_SCALE).astype(jnp.bfloat16)
    grad_queries = product("shgqk,skhw->sqhgw", grad_scores, key_row_block)
    keys_gradient = product("shgqk,sqhgw->skhw", grad_scores, query_rows)
    query_grad = inverse_rotary(
        grad_queries.reshape(local_sequences, SEQUENCE_LENGTH, QUERY_HEADS, HEAD_DIM),
        cosine_table,
        sine_table,
    )
    query_grad = query_grad.astype(jnp.bfloat16).reshape(token_rows, QUERY_HEADS * HEAD_DIM)
    key_gradient = (
        inverse_rotary(keys_gradient, cosine_table, sine_table)
        .astype(jnp.bfloat16)
        .reshape(token_rows, KEY_VALUE_HEADS * HEAD_DIM)
    )
    value_gradient = values_gradient.astype(jnp.bfloat16).reshape(
        token_rows, KEY_VALUE_HEADS * HEAD_DIM
    )
    query_wgrad = matrix_multiply(attention_input.T, query_grad)
    key_wgrad = matrix_multiply(attention_input.T, key_gradient)
    value_wgrad = matrix_multiply(attention_input.T, value_gradient)
    grad_attn_input = (
        matrix_multiply(query_grad, query_mat.T)
        + matrix_multiply(key_gradient, key_matrix.T)
        + matrix_multiply(value_gradient, value_matrix.T)
    )
    grad_normed, gain_grad = normalize_back(grad_attn_input, normed, factor, gain_vec)
    return (grad_hidden + grad_normed, gain_grad, query_wgrad, key_wgrad, value_wgrad, out_grad)


def route_weights(expert_input, router_mat, routes):
    logits = matrix_multiply(expert_input, router_mat)
    chosen_hot = (
        routes[:, :, None] == jnp.arange(router_mat.shape[1], dtype=jnp.int32)[None, None, :]
    ).astype(jnp.float32)
    chosen = jnp.sum(chosen_hot * logits[:, None, :], -1)
    return (jax.nn.softmax(chosen, -1), chosen_hot)


def route_back(route_prob, grad_prob, chosen_hot):
    grad_chosen = route_prob * (grad_prob - jnp.sum(route_prob * grad_prob, -1, keepdims=True))
    return jnp.sum(chosen_hot * grad_chosen[:, :, None], 1).astype(jnp.bfloat16)


def expert_forward(owner_rows, gate_mat, up_mat, down_mat):
    gate_pre = product("erd,edf->erf", owner_rows, gate_mat)
    up_pre = product("erd,edf->erf", owner_rows, up_mat)
    gate_sig = jax.nn.sigmoid(gate_pre)
    gate_act = gate_pre * gate_sig
    inner_acts = (gate_act * up_pre).astype(jnp.bfloat16)
    expert_out = product("erf,efd->erd", inner_acts, down_mat).astype(jnp.bfloat16)
    return (expert_out, (gate_pre, up_pre, gate_sig, gate_act, inner_acts))


def expert_backward(grad_rows, owner_rows, kept_acts, gate_mat, up_mat, down_mat):
    gate_pre, up_pre, gate_sig, gate_act, inner_acts = kept_acts
    grad_inner = product("erd,efd->erf", grad_rows, down_mat)
    down_grad = product("erf,erd->efd", inner_acts, grad_rows)
    silu_slope = gate_sig * (1.0 + gate_pre * (1.0 - gate_sig))
    grad_gate = (grad_inner * up_pre * silu_slope).astype(jnp.bfloat16)
    grad_up = (grad_inner * gate_act).astype(jnp.bfloat16)
    gate_grad = product("erd,erf->edf", owner_rows, grad_gate)
    up_grad = product("erd,erf->edf", owner_rows, grad_up)
    grad_owner_rows = product("erf,edf->erd", grad_gate, gate_mat) + product(
        "erf,edf->erd", grad_up, up_mat
    )
    return (grad_owner_rows.astype(jnp.bfloat16), gate_grad, up_grad, down_grad)


def gather_dp(local_part):
    dp_count = lax.axis_size("dp")
    if dp_count != 2:
        return lax.all_gather(local_part, "dp", axis=0, tiled=True)
    other = lax.ppermute(local_part, "dp", [(0, 1), (1, 0)])
    first = lax.axis_index("dp") == 0
    return jnp.concatenate(
        [jnp.where(first, local_part, other), jnp.where(first, other, local_part)], 0
    )


def scatter_dp(partial, axis):
    dp_count = lax.axis_size("dp")
    rounded = partial.astype(jnp.bfloat16)
    if dp_count != 2:
        return lax.psum_scatter(rounded, "dp", scatter_dimension=axis, tiled=True).astype(
            jnp.float32
        )
    low, high = jnp.split(rounded, 2, axis)
    first = lax.axis_index("dp") == 0
    arrived = lax.ppermute(jnp.where(first, high, low), "dp", [(0, 1), (1, 0)])
    return jnp.where(first, low, high).astype(jnp.float32) + arrived.astype(jnp.float32)


def two_parts(values):
    high = lax.reduce_precision(values, 8, 7)
    return (high.astype(jnp.bfloat16), (values - high).astype(jnp.bfloat16))


def shards(
    tokens,
    segments,
    routes,
    first_gain,
    query_weight,
    key_projection_weight,
    value_projection_weight,
    out_weight,
    second_gain,
    router_weight,
    gate_weight,
    up_weight,
    down_weight,
    cotangent,
):
    token_rows, model_width = tokens.shape
    top_count = routes.shape[1]
    expert_count = router_weight.shape[1]
    owner_count = lax.axis_size("expert")
    local_count = gate_weight.shape[0]
    key_width = key_projection_weight.shape[1]
    query_width = query_weight.shape[1]
    capacity = 5 * token_rows * top_count // (4 * expert_count)
    row_part = router_weight.shape[0]

    small = jnp.concatenate(
        [router_weight, first_gain[:, None], second_gain[:, None]], 1
    )
    small_mat = gather_dp(small)
    router_mat = small_mat[:, :expert_count]
    gain_first = small_mat[:, expert_count]
    gain_second = small_mat[:, expert_count + 1]
    query_mat = gather_dp(query_weight)
    key_matrix = gather_dp(key_projection_weight)
    value_matrix = gather_dp(value_projection_weight)
    out_mat = gather_dp(out_weight)

    routes_all = lax.all_gather(routes, "expert")
    cotangent_all = lax.all_gather(cotangent, "expert")

    mine = lax.axis_index("expert") * local_count + jnp.arange(local_count, dtype=jnp.int32)
    hit = jnp.any(routes_all[None] == mine[:, None, None, None], -1)
    before = (
        jnp.arange(token_rows)[:, None] < jnp.arange(token_rows)[None, :]
    ).astype(jnp.bfloat16)
    rank = product("lst,tu->lsu", hit.astype(jnp.bfloat16), before).astype(jnp.int32)
    slot = jnp.where(hit, rank, -1)
    picked = slot[:, :, None, :] == jnp.arange(capacity, dtype=jnp.int32)[None, None, :, None]
    pick = picked.astype(jnp.bfloat16)

    def rows_of(gathered):
        rows = product("lsct,std->lscd", pick, gathered)
        return rows.reshape(local_count, owner_count * capacity, model_width)

    def tokens_of(rows):
        shaped = rows.reshape(local_count, owner_count, capacity, rows.shape[-1])
        return product("lsct,lscd->std", pick, shaped).astype(jnp.bfloat16)

    hidden, saved = mixer_forward(
        tokens, segments, gain_first, query_mat, key_matrix, value_matrix, out_mat
    )
    normed_second, factor_second, expert_input = normalize(hidden, gain_second)
    input_all = lax.all_gather(expert_input, "expert")
    route_prob, chosen_hot = route_weights(expert_input, router_mat, routes)
    dense_prob = jnp.sum(chosen_hot * route_prob[:, :, None], 1)
    prob_all = lax.all_gather(dense_prob, "expert")

    column = jnp.arange(expert_count, dtype=jnp.int32)
    my_column = (mine[:, None] == column[None, :]).astype(jnp.float32)
    my_prob = jnp.sum(prob_all[None] * my_column[:, None, None, :], -1)
    row_prob = jnp.sum(jnp.where(picked, my_prob[:, :, None, :], 0.0), -1).reshape(
        local_count, owner_count * capacity, 1
    )

    owner_rows = rows_of(input_all).astype(jnp.bfloat16)
    cotangent_rows = rows_of(cotangent_all).astype(jnp.bfloat16).astype(jnp.float32)
    expert_out, kept_acts = expert_forward(owner_rows, gate_weight, up_weight, down_weight)
    expert_out = expert_out.astype(jnp.float32)
    weighted = (row_prob * expert_out).astype(jnp.bfloat16)
    row_grad_prob = jnp.sum(expert_out * cotangent_rows, -1).reshape(
        local_count, owner_count, capacity
    )
    token_grad_prob = jnp.sum(jnp.where(picked, row_grad_prob[..., None], 0.0), 2)
    dense_grad_prob = jnp.sum(
        token_grad_prob[..., None] * my_column[:, None, None, :], 0
    )
    high_part, low_part = two_parts(dense_grad_prob)
    forward_send = jnp.concatenate([tokens_of(weighted), high_part, low_part], -1)
    forward_sum = lax.psum_scatter(
        forward_send.reshape(owner_count * token_rows, -1),
        "expert",
        scatter_dimension=0,
        tiled=True,
    ).astype(jnp.float32)
    output = (hidden + forward_sum[:, :model_width]).astype(jnp.bfloat16)
    dense_back = (
        forward_sum[:, model_width : model_width + expert_count]
        + forward_sum[:, model_width + expert_count :]
    )
    grad_prob = jnp.sum(chosen_hot * dense_back[:, None, :], -1)
    grad_output = cotangent.astype(jnp.float32)

    grad_rows = (row_prob * cotangent_rows).astype(jnp.bfloat16)
    grad_owner_rows, gate_grad, up_grad, down_grad = expert_backward(
        grad_rows, owner_rows, kept_acts, gate_weight, up_weight, down_weight
    )
    backward_sum = lax.psum_scatter(
        tokens_of(grad_owner_rows).reshape(owner_count * token_rows, -1),
        "expert",
        scatter_dimension=0,
        tiled=True,
    )
    expert_shares = (
        scatter_dp(gate_grad, 1),
        scatter_dp(up_grad, 1),
        scatter_dp(down_grad, 2),
    )
    router_grad = route_back(route_prob, grad_prob, chosen_hot)
    grad_expert_input = backward_sum.astype(jnp.float32) + matrix_multiply(
        router_grad, router_mat.T
    )
    router_wgrad = matrix_multiply(expert_input.T, router_grad)
    grad_normed, second_gain_grad = normalize_back(
        grad_expert_input, normed_second, factor_second, gain_second
    )
    grad_hidden = grad_output + grad_normed
    grad_tokens, first_gain_grad, query_wgrad, key_wgrad, value_wgrad, out_wgrad = mixer_backward(
        grad_hidden, saved, gain_first, query_mat, key_matrix, value_matrix, out_mat
    )

    def total(partial):
        piece = lax.psum_scatter(
            partial.astype(jnp.bfloat16), ("dp", "expert"), scatter_dimension=0, tiled=True
        )
        return lax.all_gather(piece, "expert", axis=0, tiled=True)

    out_share = total(out_wgrad).astype(jnp.float32)
    joined = total(
        jnp.concatenate(
            [
                query_wgrad,
                key_wgrad,
                value_wgrad,
                router_wgrad,
                first_gain_grad[:, None],
                second_gain_grad[:, None],
            ],
            1,
        )
    ).astype(jnp.float32)
    cuts = []
    start = 0
    for width in (query_width, key_width, key_width, expert_count, 1, 1):
        cuts.append(joined[:, start : start + width])
        start += width
    query_share, key_share, value_share, router_share, first_share, second_share = cuts
    return (
        output,
        grad_tokens,
        first_share.reshape(row_part),
        query_share,
        key_share,
        value_share,
        out_share,
        second_share.reshape(row_part),
        router_share,
        expert_shares[0],
        expert_shares[1],
        expert_shares[2],
    )


def solution(mesh):
    placed = (
        P(("dp", "expert"), None),
        P(("dp", "expert")),
        P(("dp", "expert"), None),
        P("dp"),
        P("dp", None),
        P("dp", None),
        P("dp", None),
        P("dp", None),
        P("dp"),
        P("dp", None),
        P("expert", None, None),
        P("expert", None, None),
        P("expert", None, None),
        P(("dp", "expert"), None),
    )
    return jax.shard_map(
        shards,
        mesh=mesh,
        in_specs=placed,
        out_specs=(
            P(("dp", "expert"), None),
            P(("dp", "expert"), None),
            P("dp"),
            P("dp", None),
            P("dp", None),
            P("dp", None),
            P("dp", None),
            P("dp"),
            P("dp", None),
            P("expert", "dp", None),
            P("expert", "dp", None),
            P("expert", None, "dp"),
        ),
        check_vma=False,
    )
```

```python
import jax
import jax.numpy as jnp
from jax import lax
from jax.sharding import PartitionSpec as P

QUERY_HEADS = 16
KEY_VALUE_HEADS = 8
HEAD_DIM = 64
SEQUENCE_LENGTH = 128


EPSILON = 1e-06
SCORE_SCALE = 0.015625
ROPE_BASE = 10000.0
MASKED = -1e30


def product(pattern, left_op, right_op):
    return jnp.einsum(pattern, left_op, right_op, preferred_element_type=jnp.float32)


def matrix_multiply(left_op, right_op):
    return jnp.dot(left_op, right_op, preferred_element_type=jnp.float32)


def rope_tables(seq_len, head_size):
    positions = jnp.arange(seq_len, dtype=jnp.float32)
    exponent = jnp.arange(head_size // 2, dtype=jnp.float32) * (2.0 / head_size)
    angles = positions[:, None] * (ROPE_BASE ** (-exponent))[None, :]
    return (jnp.cos(angles)[None, :, None, :], jnp.sin(angles)[None, :, None, :])


def apply_rotary(values, cosine_table, sine_table):
    middle = values.shape[-1] // 2
    first_half = values[..., :middle]
    second_half = values[..., middle:]
    return jnp.concatenate(
        [
            first_half * cosine_table - second_half * sine_table,
            second_half * cosine_table + first_half * sine_table,
        ],
        -1,
    )


def inverse_rotary(gradient, cosine_table, sine_table):
    middle = gradient.shape[-1] // 2
    first_half = gradient[..., :middle]
    second_half = gradient[..., middle:]
    return jnp.concatenate(
        [
            first_half * cosine_table + second_half * sine_table,
            second_half * cosine_table - first_half * sine_table,
        ],
        -1,
    )


def normalize(values, gain_vec):
    factor = lax.rsqrt(jnp.mean(values * values, -1, keepdims=True) + EPSILON)
    normed = values * factor
    return (normed, factor, (normed * gain_vec).astype(jnp.bfloat16))


def normalize_back(gradient, normed, factor, gain_vec):
    gain_grad = jnp.sum(gradient * normed, 0)
    scaled = gradient * gain_vec
    return (factor * (scaled - normed * jnp.mean(scaled * normed, -1, keepdims=True)), gain_grad)


def segment_mask(segments):
    seq_len = segments.shape[1]
    causal = jnp.arange(seq_len)[:, None] >= jnp.arange(seq_len)[None, :]
    same_doc = segments[:, :, None] == segments[:, None, :]
    return (same_doc & causal[None])[:, None, None]


def score_table(query_rows, key_row_block, mask_tab):
    raw_scores = product("sqhgw,skhw->shgqk", query_rows, key_row_block) * SCORE_SCALE
    return jnp.where(mask_tab, raw_scores, MASKED)


def mixer_forward(tokens, segments, gain_vec, query_mat, key_matrix, value_matrix, out_mat):
    token_rows = tokens.shape[0]
    local_sequences = token_rows // SEQUENCE_LENGTH
    query_groups = QUERY_HEADS // KEY_VALUE_HEADS
    cosine_table, sine_table = rope_tables(SEQUENCE_LENGTH, HEAD_DIM)
    mask_tab = segment_mask(segments.reshape(local_sequences, SEQUENCE_LENGTH))
    residual = tokens.astype(jnp.float32)
    normed, factor, attention_input = normalize(residual, gain_vec)
    query_rows = apply_rotary(
        matrix_multiply(attention_input, query_mat).reshape(
            local_sequences, SEQUENCE_LENGTH, QUERY_HEADS, HEAD_DIM
        ),
        cosine_table,
        sine_table,
    )
    query_rows = query_rows.astype(jnp.bfloat16).reshape(
        local_sequences, SEQUENCE_LENGTH, KEY_VALUE_HEADS, query_groups, HEAD_DIM
    )
    key_row_block = apply_rotary(
        matrix_multiply(attention_input, key_matrix).reshape(
            local_sequences, SEQUENCE_LENGTH, KEY_VALUE_HEADS, HEAD_DIM
        ),
        cosine_table,
        sine_table,
    ).astype(jnp.bfloat16)
    value_row_block = (
        matrix_multiply(attention_input, value_matrix)
        .astype(jnp.bfloat16)
        .reshape(local_sequences, SEQUENCE_LENGTH, KEY_VALUE_HEADS, HEAD_DIM)
    )
    scores = score_table(query_rows, key_row_block, mask_tab)
    row_peak = jnp.max(scores, -1, keepdims=True)
    logsum = row_peak + jnp.log(jnp.sum(jnp.exp(scores - row_peak), -1, keepdims=True))
    weights = jnp.exp(scores - logsum).astype(jnp.bfloat16)
    attended = product("shgqk,skhw->sqhgw", weights, value_row_block).astype(jnp.bfloat16)
    hidden = residual + matrix_multiply(
        attended.reshape(token_rows, QUERY_HEADS * HEAD_DIM), out_mat
    )
    saved = (
        normed,
        factor,
        attention_input,
        query_rows,
        key_row_block,
        value_row_block,
        attended,
        logsum,
        mask_tab,
        cosine_table,
        sine_table,
    )
    return (hidden, saved)


def mixer_backward(grad_hidden, saved, gain_vec, query_mat, key_matrix, value_matrix, out_mat):
    (
        normed,
        factor,
        attention_input,
        query_rows,
        key_row_block,
        value_row_block,
        attended,
        logsum,
        mask_tab,
        cosine_table,
        sine_table,
    ) = saved
    token_rows = grad_hidden.shape[0]
    local_sequences = token_rows // SEQUENCE_LENGTH
    grad_round = grad_hidden.astype(jnp.bfloat16)
    out_grad = matrix_multiply(attended.reshape(token_rows, QUERY_HEADS * HEAD_DIM).T, grad_round)
    grad_attended = (
        matrix_multiply(grad_round, out_mat.T).astype(jnp.bfloat16).reshape(query_rows.shape)
    )
    scores = score_table(query_rows, key_row_block, mask_tab)
    prob_full = jnp.exp(scores - logsum)
    values_gradient = product("shgqk,sqhgw->skhw", prob_full.astype(jnp.bfloat16), grad_attended)
    grad_weights = product("sqhgw,skhw->shgqk", grad_attended, value_row_block)
    row_delta = product("sqhgw,sqhgw->shgq", grad_attended, attended)[..., None]
    grad_scores = (prob_full * (grad_weights - row_delta) * SCORE_SCALE).astype(jnp.bfloat16)
    grad_queries = product("shgqk,skhw->sqhgw", grad_scores, key_row_block)
    keys_gradient = product("shgqk,sqhgw->skhw", grad_scores, query_rows)
    query_grad = inverse_rotary(
        grad_queries.reshape(local_sequences, SEQUENCE_LENGTH, QUERY_HEADS, HEAD_DIM),
        cosine_table,
        sine_table,
    )
    query_grad = query_grad.astype(jnp.bfloat16).reshape(token_rows, QUERY_HEADS * HEAD_DIM)
    key_gradient = (
        inverse_rotary(keys_gradient, cosine_table, sine_table)
        .astype(jnp.bfloat16)
        .reshape(token_rows, KEY_VALUE_HEADS * HEAD_DIM)
    )
    value_gradient = values_gradient.astype(jnp.bfloat16).reshape(
        token_rows, KEY_VALUE_HEADS * HEAD_DIM
    )
    query_wgrad = matrix_multiply(attention_input.T, query_grad)
    key_wgrad = matrix_multiply(attention_input.T, key_gradient)
    value_wgrad = matrix_multiply(attention_input.T, value_gradient)
    grad_attn_input = (
        matrix_multiply(query_grad, query_mat.T)
        + matrix_multiply(key_gradient, key_matrix.T)
        + matrix_multiply(value_gradient, value_matrix.T)
    )
    grad_normed, gain_grad = normalize_back(grad_attn_input, normed, factor, gain_vec)
    return (grad_hidden + grad_normed, gain_grad, query_wgrad, key_wgrad, value_wgrad, out_grad)


def route_weights(expert_input, router_mat, routes):
    logits = matrix_multiply(expert_input, router_mat)
    chosen_hot = (
        routes[:, :, None] == jnp.arange(router_mat.shape[1], dtype=jnp.int32)[None, None, :]
    ).astype(jnp.float32)
    chosen = jnp.sum(chosen_hot * logits[:, None, :], -1)
    return (jax.nn.softmax(chosen, -1), chosen_hot)


def route_back(route_prob, grad_prob, chosen_hot):
    grad_chosen = route_prob * (grad_prob - jnp.sum(route_prob * grad_prob, -1, keepdims=True))
    return jnp.sum(chosen_hot * grad_chosen[:, :, None], 1).astype(jnp.bfloat16)


def expert_forward(owner_rows, gate_mat, up_mat, down_mat):
    gate_pre = product("erd,edf->erf", owner_rows, gate_mat)
    up_pre = product("erd,edf->erf", owner_rows, up_mat)
    gate_sig = jax.nn.sigmoid(gate_pre)
    gate_act = gate_pre * gate_sig
    inner_acts = (gate_act * up_pre).astype(jnp.bfloat16)
    expert_out = product("erf,efd->erd", inner_acts, down_mat).astype(jnp.bfloat16)
    return (expert_out, (gate_pre, up_pre, gate_sig, gate_act, inner_acts))


def expert_backward(grad_rows, owner_rows, kept_acts, gate_mat, up_mat, down_mat):
    gate_pre, up_pre, gate_sig, gate_act, inner_acts = kept_acts
    grad_inner = product("erd,efd->erf", grad_rows, down_mat)
    down_grad = product("erf,erd->efd", inner_acts, grad_rows)
    silu_slope = gate_sig * (1.0 + gate_pre * (1.0 - gate_sig))
    grad_gate = (grad_inner * up_pre * silu_slope).astype(jnp.bfloat16)
    grad_up = (grad_inner * gate_act).astype(jnp.bfloat16)
    gate_grad = product("erd,erf->edf", owner_rows, grad_gate)
    up_grad = product("erd,erf->edf", owner_rows, grad_up)
    grad_owner_rows = product("erf,edf->erd", grad_gate, gate_mat) + product(
        "erf,edf->erd", grad_up, up_mat
    )
    return (grad_owner_rows.astype(jnp.bfloat16), gate_grad, up_grad, down_grad)


def gather_dp(local_part):
    dp_count = lax.axis_size("dp")
    owner_count = lax.axis_size("expert")
    if dp_count != 2 or owner_count % 2:
        return lax.all_gather(local_part, "dp", axis=0, tiled=True)
    low, high = jnp.split(local_part, 2, 0)
    even = lax.axis_index("expert") % 2 == 0
    near = lax.ppermute(jnp.where(even, low, high), "dp", [(0, 1), (1, 0)])
    far = lax.ppermute(near, "expert", [(i, i ^ 1) for i in range(owner_count)])
    other = jnp.concatenate([jnp.where(even, near, far), jnp.where(even, far, near)], 0)
    first = lax.axis_index("dp") == 0
    return jnp.concatenate(
        [jnp.where(first, local_part, other), jnp.where(first, other, local_part)], 0
    )


def all_sums(partial):
    owner_count = lax.axis_size("expert")
    dp_count = lax.axis_size("dp")
    width = partial.shape[1]
    pieces = partial.astype(jnp.bfloat16).reshape(dp_count, owner_count, -1, width)
    piece = lax.psum_scatter(
        pieces.transpose(1, 0, 2, 3).reshape(-1, width), "expert", scatter_dimension=0, tiled=True
    )
    piece = scatter_dp(piece, 0).astype(jnp.bfloat16)
    return lax.all_gather(piece, "expert", axis=0, tiled=True).astype(jnp.float32)


def scatter_dp(partial, axis):
    dp_count = lax.axis_size("dp")
    rounded = partial.astype(jnp.bfloat16)
    if dp_count != 2:
        return lax.psum_scatter(rounded, "dp", scatter_dimension=axis, tiled=True).astype(
            jnp.float32
        )
    low, high = jnp.split(rounded, 2, axis)
    first = lax.axis_index("dp") == 0
    arrived = lax.ppermute(jnp.where(first, high, low), "dp", [(0, 1), (1, 0)])
    return jnp.where(first, low, high).astype(jnp.float32) + arrived.astype(jnp.float32)


def shards(
    tokens,
    segments,
    routes,
    first_gain,
    query_weight,
    key_projection_weight,
    value_projection_weight,
    out_weight,
    second_gain,
    router_weight,
    gate_weight,
    up_weight,
    down_weight,
    cotangent,
):
    token_rows, model_width = tokens.shape
    top_count = routes.shape[1]
    expert_count = router_weight.shape[1]
    owner_count = lax.axis_size("expert")
    local_count = gate_weight.shape[0]
    key_width = key_projection_weight.shape[1]
    query_width = query_weight.shape[1]
    capacity = 5 * token_rows * top_count // (4 * expert_count)
    row_part = router_weight.shape[0]

    small = jnp.concatenate(
        [router_weight, first_gain[:, None], second_gain[:, None]], 1
    )
    small_mat = gather_dp(small)
    router_mat = small_mat[:, :expert_count]
    gain_first = small_mat[:, expert_count]
    gain_second = small_mat[:, expert_count + 1]
    joined_mat = gather_dp(
        jnp.concatenate([query_weight, key_projection_weight, value_projection_weight], 1)
    )
    query_mat = joined_mat[:, :query_width]
    key_matrix = joined_mat[:, query_width : query_width + key_width]
    value_matrix = joined_mat[:, query_width + key_width :]
    out_mat = gather_dp(out_weight)

    routes_all = lax.all_gather(routes, "expert")
    cotangent_all = lax.all_gather(cotangent, "expert")

    mine = lax.axis_index("expert") * local_count + jnp.arange(local_count, dtype=jnp.int32)
    hit = jnp.any(routes_all[None] == mine[:, None, None, None], -1)
    before = (
        jnp.arange(token_rows)[:, None] < jnp.arange(token_rows)[None, :]
    ).astype(jnp.bfloat16)
    rank = product("lst,tu->lsu", hit.astype(jnp.bfloat16), before).astype(jnp.int32)
    slot = jnp.where(hit, rank, -1)
    picked = slot[:, :, None, :] == jnp.arange(capacity, dtype=jnp.int32)[None, None, :, None]
    pick = picked.astype(jnp.bfloat16)

    def rows_of(gathered):
        rows = product("lsct,std->lscd", pick, gathered)
        return rows.reshape(local_count, owner_count * capacity, model_width)

    own_hot = (routes[:, :, None] == jnp.arange(expert_count, dtype=jnp.int32)).any(1)
    own_rank = matrix_multiply(before.T, own_hot.astype(jnp.bfloat16)).astype(jnp.int32)
    own_slot = jnp.where(own_hot, own_rank, -1)
    own_pick = (
        own_slot[:, :, None] == jnp.arange(capacity, dtype=jnp.int32)[None, None, :]
    ).astype(jnp.bfloat16)

    def send_back(rows):
        shaped = rows.reshape(local_count, owner_count, capacity, model_width)
        return lax.all_to_all(
            shaped.transpose(1, 0, 2, 3).reshape(expert_count, capacity, model_width),
            "expert",
            split_axis=0,
            concat_axis=0,
            tiled=True,
        )

    def sum_back(returned):
        flat = returned.reshape(expert_count * capacity, model_width)
        return matrix_multiply(own_pick.reshape(token_rows, expert_count * capacity), flat)

    hidden, saved = mixer_forward(
        tokens, segments, gain_first, query_mat, key_matrix, value_matrix, out_mat
    )
    normed_second, factor_second, expert_input = normalize(hidden, gain_second)
    input_all = lax.all_gather(expert_input, "expert")
    route_prob, chosen_hot = route_weights(expert_input, router_mat, routes)
    dense_prob = jnp.sum(chosen_hot * route_prob[:, :, None], 1)
    prob_all = lax.all_gather(dense_prob, "expert")

    column = jnp.arange(expert_count, dtype=jnp.int32)
    my_column = (mine[:, None] == column[None, :]).astype(jnp.float32)
    my_prob = jnp.sum(prob_all[None] * my_column[:, None, None, :], -1)
    row_prob = jnp.sum(jnp.where(picked, my_prob[:, :, None, :], 0.0), -1).reshape(
        local_count, owner_count * capacity, 1
    )

    owner_rows = rows_of(input_all).astype(jnp.bfloat16)
    cotangent_rows = rows_of(cotangent_all).astype(jnp.bfloat16).astype(jnp.float32)
    expert_out, kept_acts = expert_forward(owner_rows, gate_weight, up_weight, down_weight)
    expert_out = expert_out.astype(jnp.float32)
    weighted = (row_prob * expert_out).astype(jnp.bfloat16)
    row_grad_prob = jnp.sum(expert_out * cotangent_rows, -1).reshape(
        local_count, owner_count, capacity
    )
    token_grad_prob = jnp.sum(jnp.where(picked, row_grad_prob[..., None], 0.0), 2)
    back_prob = lax.all_to_all(
        token_grad_prob.transpose(1, 0, 2).reshape(expert_count, token_rows),
        "expert",
        split_axis=0,
        concat_axis=0,
        tiled=True,
    )
    grad_prob = jnp.sum(chosen_hot * back_prob.T[:, None, :], -1)
    grad_output = cotangent.astype(jnp.float32)

    grad_rows = (row_prob * cotangent_rows).astype(jnp.bfloat16)
    grad_owner_rows, gate_grad, up_grad, down_grad = expert_backward(
        grad_rows, owner_rows, kept_acts, gate_weight, up_weight, down_weight
    )
    grad_back = send_back(grad_owner_rows)
    expert_shares = (
        scatter_dp(gate_grad, 1),
        scatter_dp(up_grad, 1),
        scatter_dp(down_grad, 2),
    )
    grad_back, expert_shares, weighted = lax.optimization_barrier(
        (grad_back, expert_shares, weighted)
    )
    forward_back = send_back(weighted)
    output = (hidden + sum_back(forward_back)).astype(jnp.bfloat16)
    backward_sum = sum_back(grad_back)
    router_grad = route_back(route_prob, grad_prob, chosen_hot)
    grad_expert_input = backward_sum + matrix_multiply(
        router_grad, router_mat.T
    )
    router_wgrad = matrix_multiply(router_grad.T, expert_input)
    grad_normed, second_gain_grad = normalize_back(
        grad_expert_input, normed_second, factor_second, gain_second
    )
    grad_hidden = grad_output + grad_normed
    grad_tokens, first_gain_grad, query_wgrad, key_wgrad, value_wgrad, out_wgrad = mixer_backward(
        grad_hidden, saved, gain_first, query_mat, key_matrix, value_matrix, out_mat
    )

    out_share = all_sums(out_wgrad)
    joined = all_sums(jnp.concatenate([query_wgrad, key_wgrad, value_wgrad], 1))
    query_share = joined[:, :query_width]
    key_share = joined[:, query_width : query_width + key_width]
    value_share = joined[:, query_width + key_width :]
    extras = jnp.concatenate(
        [router_wgrad, first_gain_grad[None, :], second_gain_grad[None, :]], 0
    )
    extras = lax.psum(extras.astype(jnp.bfloat16), ("dp", "expert"))
    extras = lax.dynamic_slice_in_dim(
        extras, lax.axis_index("dp") * row_part, row_part, 1
    ).astype(jnp.float32)
    router_share = extras[:expert_count].T
    first_share = extras[expert_count]
    second_share = extras[expert_count + 1]
    return (
        output,
        grad_tokens,
        first_share,
        query_share,
        key_share,
        value_share,
        out_share,
        second_share,
        router_share,
        expert_shares[0],
        expert_shares[1],
        expert_shares[2],
    )


def solution(mesh):
    placed = (
        P(("dp", "expert"), None),
        P(("dp", "expert")),
        P(("dp", "expert"), None),
        P("dp"),
        P("dp", None),
        P("dp", None),
        P("dp", None),
        P("dp", None),
        P("dp"),
        P("dp", None),
        P("expert", None, None),
        P("expert", None, None),
        P("expert", None, None),
        P(("dp", "expert"), None),
    )
    return jax.shard_map(
        shards,
        mesh=mesh,
        in_specs=placed,
        out_specs=(
            P(("dp", "expert"), None),
            P(("dp", "expert"), None),
            P("dp"),
            P("dp", None),
            P("dp", None),
            P("dp", None),
            P("dp", None),
            P("dp"),
            P("dp", None),
            P("expert", "dp", None),
            P("expert", "dp", None),
            P("expert", None, "dp"),
        ),
        check_vma=False,
    )
```
